32 devices in a mesh: rows: 8 (over y, x, core), feat: 4 (over z).
Axes of the slice: x: 2, y: 2, z: 4, core: 2. Of those that a mesh axis runs over, the one named last changes fastest.
Arguments:
- activations: bfloat16 [256, 96, 8192], P('rows', None, 'feat'), may hold values from -6 to 6
- out_grads: bfloat16 [256, 96, 8192], P('rows', None, 'feat'), may hold values from -6 to 6
- proj_in: bfloat16 [8192, 128], P('feat'), may hold values from -0.0625 to 0.0625
- proj_out: bfloat16 [8192, 128], P('feat'), may hold values from -0.0625 to 0.0625
- lengths: int32 [256], P('rows'), may hold values from 12 to 96
- hess_tiles: bfloat16 [16, 1024, 1024], P('feat'), may hold values from -3 to 3
- train_grads: bfloat16 [16384, 16384], P('rows', 'feat'), may hold values from -6 to 6
Outputs:
- scores: float32 [256, 16384], P('feat', 'rows')
The draws below stay inside these ranges and needn't reach their ends.
All inputs are finite; a program needn't handle non-finite values.
Results may differ from the reference program's by a relative error of at most 0.0057.
Values may be sent and summed in bfloat16 or wider, within the bound.
No kernel may reach another device: no remote copies, remote signals or barrier semaphores. Data moves between devices by JAX's collectives and lax.ppermute only.
A program may use at most 128 MiB of HBM per device.

```python
import jax
import jax.numpy as jnp
from jax import lax

D = 8192
R = 128
BLK = 1024
SEQ = 96
QUERIES = 256
NTRAIN = 16384
FEATS = 16384
NBLK = 16


def draw_lengths(key, part):
    values = jax.random.randint(key, (QUERIES,), SEQ // 8, SEQ + 1)
    return values.at[0].set(SEQ).at[1].set(SEQ // 8).astype(jnp.int32)


def draw_hess_tiles(key, part):
    key_diag, key_off = jax.random.split(jax.random.fold_in(key, 11))
    diag = jax.random.uniform(key_diag, (NBLK, BLK), minval=1.0, maxval=2.0)
    off = jax.random.normal(key_off, (NBLK, BLK, BLK)) * (0.7 / jnp.sqrt(jnp.float32(BLK)))
    tiles = off + diag[:, :, None] * jnp.eye(BLK, dtype=jnp.float32)[None, :, :]
    return jnp.clip(tiles, -3.0, 3.0).astype(jnp.bfloat16)


def steps_of(own_key, shape, cuts, smallest, top_value):
    loudness = 1.0
    for dim, blocks in cuts:
        steps = jax.random.uniform(jax.random.fold_in(jax.random.fold_in(own_key, 6), dim), (blocks,), jnp.float32, smallest / len(cuts), top_value / len(cuts))
        loudness = loudness * jnp.repeat(jnp.exp(steps), shape[dim] // blocks).reshape((-1,) + (1,) * (len(shape) - 1 - dim))
    return loudness


def scatter_about(key, extent, scale, limit, cuts=(), kind=jnp.bfloat16):
    result = scale * jax.random.normal(key, extent, jnp.float32)
    if cuts:
        result = result * steps_of(key, extent, cuts, -0.22, 0.18)
    return jnp.clip(result, -limit, limit).astype(kind)


def setup_inputs(seed: int = 0) -> dict:
    splits = jax.random.split(jax.random.key(seed), 8)
    return {
        "activations": scatter_about(splits[0], (QUERIES, SEQ, D), 1.0, 6.0, ((0, 8), (2, 4))),
        "out_grads": scatter_about(splits[1], (QUERIES, SEQ, D), 1.0, 6.0, ((0, 8), (2, 4))),
        "proj_in": scatter_about(splits[2], (D, R), D ** -0.5, 0.0625, ((0, 4),)),
        "proj_out": scatter_about(splits[3], (D, R), D ** -0.5, 0.0625, ((0, 4),)),
        "lengths": draw_lengths(jax.random.fold_in(splits[7], 71), 0),
        "hess_tiles": draw_hess_tiles(jax.random.fold_in(splits[7], 71), 0),
        "train_grads": scatter_about(splits[6], (NTRAIN, FEATS), 1.0, 6.0, ((0, 8), (1, 4))),
    }


def reference(activations, out_grads, proj_in, proj_out, lengths, hess_tiles, train_grads):
    positions = jnp.arange(SEQ, dtype=jnp.int32)
    mask = (positions[None, :] < lengths[:, None]).astype(jnp.float32)[:, :, None]
    act_full = jnp.dot(activations.reshape(QUERIES * SEQ, D), proj_in, preferred_element_type=jnp.float32)
    grad_full = jnp.dot(out_grads.reshape(QUERIES * SEQ, D), proj_out, preferred_element_type=jnp.float32)
    act_low = (act_full.reshape(QUERIES, SEQ, R) * mask).astype(jnp.bfloat16)
    grad_low = (grad_full.reshape(QUERIES, SEQ, R) * mask).astype(jnp.bfloat16)
    kron = jnp.einsum('qti,qtj->qij', grad_low.astype(jnp.float32), act_low.astype(jnp.float32))
    kron = (kron * (1.0 / jnp.sqrt(jnp.float32(SEQ)))).astype(jnp.bfloat16)
    kron_blocks = kron.reshape(QUERIES, NBLK, BLK)
    precond = jnp.einsum('qbk,bkl->qbl', kron_blocks.astype(jnp.float32), hess_tiles.astype(jnp.float32))
    precond = precond.astype(jnp.bfloat16).reshape(QUERIES, FEATS)
    scores = lax.dot_general(precond, train_grads, (((1,), (1,)), ((), ())), preferred_element_type=jnp.float32)
    return scores * (1.0 / R)
```

```python
import functools

import jax
import jax.numpy as jnp
from jax import lax
from jax.experimental import pallas as pl
from jax.experimental.pallas import tpu as pltpu
from jax.sharding import PartitionSpec as P

BF = jnp.bfloat16
F32 = jnp.float32
TOK = 16
HBM = pl.BlockSpec(memory_space=pl.ANY)
VMEM = pl.BlockSpec(memory_space=pltpu.VMEM)
SMEM = pl.BlockSpec(memory_space=pltpu.SMEM)


def blocks_of(length):
    return (length + (TOK - 1)) >> (TOK.bit_length() - 1)


def proj_kernel(shift, nz, nq, chunk, act, grad, w_in, w_out, lengths, out, abuf, gbuf, sems):
    owner = lax.rem(lax.axis_index("feat") + shift, nz)
    first = owner * nq
    per = chunk // TOK
    offset = jnp.int32(0)
    for j in range(nq):
        count = blocks_of(lengths[first + j])

        def issue(k, carry, j=j, offset=offset):
            src = pl.ds(pl.multiple_of(k * TOK, TOK), TOK)
            dst = pl.ds(pl.multiple_of((offset + k) * TOK, TOK), TOK)
            sem = lax.div(offset + k, per)
            pltpu.make_async_copy(act.at[first + j, src, :], abuf.at[dst, :], sems.at[0, sem]).start()
            pltpu.make_async_copy(grad.at[first + j, src, :], gbuf.at[dst, :], sems.at[1, sem]).start()
            return carry

        lax.fori_loop(0, count, issue, 0)
        offset = offset + count
    total = offset

    def step(i, carry):
        here = jnp.minimum(per, total - i * per)

        def drain(which, buf):
            def one(k, c):
                pltpu.make_async_copy(act.at[0, pl.ds(0, TOK), :], buf.at[pl.ds(0, TOK), :], sems.at[which, i]).wait()
                return c

            lax.fori_loop(0, here, one, 0)

        rows = pl.ds(pl.multiple_of(i * chunk, chunk), chunk)
        rank = w_in.shape[1]
        drain(0, abuf)
        out[rows, 0:rank] = jnp.dot(abuf[rows, :], w_in[...], preferred_element_type=F32).astype(out.dtype)
        drain(1, gbuf)
        out[rows, rank : 2 * rank] = jnp.dot(gbuf[rows, :], w_out[...], preferred_element_type=F32).astype(out.dtype)
        return carry

    lax.fori_loop(0, lax.div(total + (per - 1), per), step, 0)


def project(shift, nz, act, grad, w_in, w_out, lengths, dtype):
    queries, seq, width = act.shape
    rank = w_in.shape[1]
    nq = queries // nz
    rows = nq * seq
    chunk = rows
    for c in (256, 128, 192, 96, 64, 32, 16):
        if rows % c == 0:
            chunk = c
            break
    return pl.pallas_call(
        functools.partial(proj_kernel, shift, nz, nq, chunk),
        out_shape=jax.ShapeDtypeStruct((rows, 2 * rank), dtype),
        in_specs=[HBM, HBM, VMEM, VMEM, SMEM],
        out_specs=VMEM,
        scratch_shapes=[
            pltpu.VMEM((rows, width), BF),
            pltpu.VMEM((rows, width), BF),
            pltpu.SemaphoreType.DMA((2, rows // chunk)),
        ],
        compiler_params=pltpu.CompilerParams(vmem_limit_bytes=24 << 20),
        cost_estimate=pl.CostEstimate(
            flops=4 * rows * width * rank, bytes_accessed=4 * rows * width, transcendentals=0
        ),
        name=f"proj{shift}",
    )(act, grad, w_in, w_out, lengths)


def kron_kernel(nz, nq, seq, lengths, *refs):
    parts, outs, scratch = refs[:nz], refs[nz : 2 * nz], refs[2 * nz]
    z = lax.axis_index("feat")
    rank = parts[0].shape[1] // 2
    offset = jnp.int32(0)
    for j in range(nq):
        length = lengths[z * nq + j]
        rows = pl.ds(pl.multiple_of(offset * TOK, TOK), seq)
        total = parts[0][rows, :].astype(F32)
        for part in parts[1:]:
            total = total + part[rows, :].astype(F32)
        tokens = lax.broadcasted_iota(jnp.int32, total.shape, 0)
        total = jnp.where(tokens < length, total, 0.0)
        high = total.astype(BF)
        low = (total - high.astype(F32)).astype(BF)
        a_hi, a_lo = high[:, :rank], low[:, :rank]
        g_hi, g_lo = high[:, rank:], low[:, rank:]
        left = jnp.concatenate([g_hi, g_hi, g_lo], axis=0)
        right = jnp.concatenate([a_hi, a_lo, a_hi], axis=0)
        outer = lax.dot_general(left, right, (((0,), (0,)), ((), ())), preferred_element_type=F32)
        scratch[:, j, :] = outer * (1.0 / jnp.sqrt(jnp.float32(seq)))
        offset = offset + blocks_of(length)
    share = rank // nz
    for shift in range(nz):
        start = lax.rem(z + shift, nz) * share
        outs[shift][...] = scratch[pl.ds(start, share), :, :].astype(BF)


def kron_of(nz, nq, seq, lengths, parts):
    rank = parts[0].shape[1] // 2
    share = rank // nz
    return pl.pallas_call(
        functools.partial(kron_kernel, nz, nq, seq),
        out_shape=[jax.ShapeDtypeStruct((share, nq, rank), BF)] * nz,
        in_specs=[SMEM] + [VMEM] * nz,
        out_specs=[VMEM] * nz,
        scratch_shapes=[pltpu.VMEM((rank, nq, rank), F32)],
        compiler_params=pltpu.CompilerParams(vmem_limit_bytes=24 << 20),
        cost_estimate=pl.CostEstimate(
            flops=6 * nq * seq * rank * rank, bytes_accessed=8 * nq * seq * rank * nz, transcendentals=0
        ),
        name="kron",
    )(lengths, *parts)


def precond_kernel(nz, hess, *refs):
    parts, out, lhs = refs[:nz], refs[nz], refs[nz + 1]
    z = lax.axis_index("feat")
    per, nq, rank = parts[0].shape
    for i in range(per):
        columns = slice(i * rank, (i + 1) * rank)
        if nq % 8 == 0:
            for shift in range(nz):
                source = lax.rem(z + (nz - shift), nz)
                lhs[pl.ds(pl.multiple_of(source * nq, nq), nq), columns] = parts[shift][i].astype(F32)
        else:
            for source in range(nz):
                value = parts[0][i].astype(F32)
                for shift in range(1, nz):
                    value = jnp.where(lax.rem(z + (nz - shift), nz) == source, parts[shift][i].astype(F32), value)
                lhs[source * nq : (source + 1) * nq, columns] = value
    out[...] = jnp.dot(lhs[...].astype(BF), hess[0], preferred_element_type=F32).astype(BF)


def precondition(nz, hess, parts):
    blocks, order, _ = hess.shape
    share, nq, rank = parts[0].shape
    per = order // rank
    queries = nq * nz
    return pl.pallas_call(
        functools.partial(precond_kernel, nz),
        grid=(blocks,),
        out_shape=jax.ShapeDtypeStruct((queries, blocks * order), BF),
        in_specs=[pl.BlockSpec((1, order, order), lambda b: (b, 0, 0))]
        + [pl.BlockSpec((per, nq, rank), lambda b: (b, 0, 0))] * nz,
        out_specs=pl.BlockSpec((queries, order), lambda b: (0, b)),
        scratch_shapes=[pltpu.VMEM((queries, order), F32)],
        compiler_params=pltpu.CompilerParams(vmem_limit_bytes=24 << 20),
        cost_estimate=pl.CostEstimate(
            flops=2 * queries * blocks * order * order, bytes_accessed=2 * blocks * order * order, transcendentals=0
        ),
        name="precond",
    )(hess, *parts)


def score_kernel(nz, nr, tile, train, *refs):
    pieces, outs, lhs, acc = refs[:4], refs[4 : 4 + nz], refs[4 + nz], refs[5 + nz]
    z, r = lax.axis_index("feat"), lax.axis_index("rows")
    half = pieces[0].shape[1]

    @pl.when(pl.program_id(0) == 0)
    def _():
        width = (nr // 2).bit_length() - 1
        for e in range(nr // 2):
            mirrored = sum(((e >> b) & 1) << (width - 1 - b) for b in range(width))
            for k, piece in enumerate(pieces):
                group = r ^ (2 * e + k // 2)
                rows = pl.ds(pl.multiple_of(group * (2 * half) + (k % 2) * half, half), half)
                lhs[rows, :] = piece[mirrored if k % 2 else e]

    acc[...] = lax.dot_general(lhs[...], train[...], (((1,), (1,)), ((), ())), preferred_element_type=F32)
    count = acc.shape[0] // nz
    for shift in range(nz):
        owner = lax.rem(z + shift, nz)
        rows = pl.ds(pl.multiple_of(owner * count, count), count)
        outs[shift][...] = acc[rows, :].astype(outs[shift].dtype)


def scores_of(nz, nr, train, slab, slabs, pieces):
    rows, width = train.shape
    rows = rows // slabs
    queries = 4 * (nr // 2) * pieces[0].shape[1]
    tile = min(512, rows)
    steps = rows // tile
    count = queries // nz
    return pl.pallas_call(
        functools.partial(score_kernel, nz, nr, tile),
        grid=(steps,),
        out_shape=[jax.ShapeDtypeStruct((count, rows), F32 if s == 0 else BF) for s in range(nz)],
        in_specs=[pl.BlockSpec((tile, width), lambda i: (slab * steps + i, 0))] + [VMEM] * 4,
        out_specs=[pl.BlockSpec((count, tile), lambda i: (0, i))] * nz,
        scratch_shapes=[pltpu.VMEM((queries, width), BF), pltpu.VMEM((queries, tile), F32)],
        compiler_params=pltpu.CompilerParams(vmem_limit_bytes=28 << 20),
        cost_estimate=pl.CostEstimate(
            flops=2 * queries * rows * width, bytes_accessed=2 * rows * width, transcendentals=0
        ),
        name=f"scores{slab}",
    )(train, *pieces)


def on_device(nz, nr, activations, out_grads, proj_in, proj_out, lengths, hess_tiles, train_grads):
    queries, seq, _ = activations.shape
    rank = proj_in.shape[1]
    nq = queries // nz

    def to_shift(x, shift):
        return lax.ppermute(x, "feat", [(i, (i + shift) % nz) for i in range(nz)])

    def across(x, bit):
        return lax.ppermute(x, "rows", [(i, i ^ bit) for i in range(nr)])

    order = sorted(range(1, nz), key=lambda s: -min(s, nz - s))
    received = {}
    for shift in order:
        part = project(shift, nz, activations, out_grads, proj_in, proj_out, lengths, BF)
        received[shift] = to_shift(part, shift)
    own = project(0, nz, activations, out_grads, proj_in, proj_out, lengths, F32)
    krons = kron_of(nz, nq, seq, lengths, [own] + [received[s] for s in range(1, nz)])
    pieces = [krons[0]] + [to_shift(krons[s], s) for s in range(1, nz)]
    precond = precondition(nz, hess_tiles, pieces)

    half = queries // 2
    bits = [1 << b for b in range(1, nr.bit_length() - 1)]
    first, second = precond[None, :half], precond[None, half:]
    for bit, other in zip(bits, reversed(bits), strict=True):
        got_first, got_second = across(first, bit), across(second, other)
        first = jnp.concatenate([first, got_first], axis=0)
        second = jnp.concatenate([second, got_second], axis=0)
    gathered = [first, second, across(first, 1), across(second, 1)]

    slabs = 2
    columns = []
    for slab in range(slabs):
        parts = scores_of(nz, nr, train_grads, slab, slabs, gathered)
        total = parts[0]
        for shift in order:
            total = total + to_shift(parts[shift], shift).astype(F32)
        columns.append(total * (1.0 / rank))
    return jnp.concatenate(columns, axis=1)


def solution(mesh):
    nz, nr = mesh.shape["feat"], mesh.shape["rows"]
    return jax.shard_map(
        functools.partial(on_device, nz, nr),
        mesh=mesh,
        in_specs=(
            P("rows", None, "feat"),
            P("rows", None, "feat"),
            P("feat", None),
            P("feat", None),
            P("rows"),
            P("feat", None, None),
            P("rows", "feat"),
        ),
        out_specs=P("feat", "rows"),
        check_vma=False,
    )
```

```python
import functools

import jax
import jax.numpy as jnp
from jax import lax
from jax.experimental import pallas as pl
from jax.experimental.pallas import tpu as pltpu
from jax.sharding import PartitionSpec as P

BF = jnp.bfloat16
F32 = jnp.float32
TOK = 16
HALVES = 2
HBM = pl.BlockSpec(memory_space=pltpu.HBM)
VMEM = pl.BlockSpec(memory_space=pltpu.VMEM)
SMEM = pl.BlockSpec(memory_space=pltpu.SMEM)


def blocks_of(length):
    return (length + (TOK - 1)) >> (TOK.bit_length() - 1)


def params(mib):
    return pltpu.CompilerParams(vmem_limit_bytes=mib << 20)


def proj_kernel(relative, nz, nq, half, chunk, act, grad, w_in, w_out, lengths, out, abuf, gbuf, win, wout, sems, wsem):
    z = lax.axis_index("feat")
    per = chunk // TOK
    load_in = pltpu.make_async_copy(w_in, win, wsem.at[0])
    load_out = pltpu.make_async_copy(w_out, wout, wsem.at[1])
    load_in.start()
    load_out.start()
    totals = []
    for n, e in enumerate(relative):
        first = (half * nz + (z ^ e)) * nq
        offset = jnp.int32(0)
        for j in range(nq):
            count = blocks_of(lengths[first + j])

            def issue(k, carry, n=n, j=j, first=first, offset=offset):
                src = pl.ds(pl.multiple_of(k * TOK, TOK), TOK)
                dst = pl.ds(pl.multiple_of((offset + k) * TOK, TOK), TOK)
                sem = lax.div(offset + k, per)
                pltpu.make_async_copy(act.at[first + j, src, :], abuf.at[n, dst, :], sems.at[0, n, sem]).start()
                pltpu.make_async_copy(grad.at[first + j, src, :], gbuf.at[n, dst, :], sems.at[1, n, sem]).start()
                return carry

            lax.fori_loop(0, count, issue, 0)
            offset = offset + count
        totals.append(offset)
    load_in.wait()
    load_out.wait()
    rank = w_in.shape[1]
    for n in range(len(relative)):
        total = totals[n]

        def step(i, carry, n=n, total=total):
            here = jnp.minimum(per, total - i * per)

            def drain(which, buf):
                def one(k, c):
                    pltpu.make_async_copy(
                        act.at[0, pl.ds(0, TOK), :], buf.at[n, pl.ds(0, TOK), :], sems.at[which, n, i]
                    ).wait()
                    return c

                lax.fori_loop(0, here, one, 0)

            rows = pl.ds(pl.multiple_of(i * chunk, chunk), chunk)
            drain(0, abuf)
            out[n, rows, 0:rank] = jnp.dot(abuf[n, rows, :], win[...], preferred_element_type=F32).astype(out.dtype)
            drain(1, gbuf)
            out[n, rows, rank : 2 * rank] = jnp.dot(gbuf[n, rows, :], wout[...], preferred_element_type=F32).astype(
                out.dtype
            )
            return carry

        lax.fori_loop(0, lax.div(total + (per - 1), per), step, 0)


def project(relative, nz, half, act, grad, w_in, w_out, lengths, dtype):
    queries, seq, width = act.shape
    rank = w_in.shape[1]
    nq = queries // (nz * HALVES)
    rows = nq * seq
    chunk = next(c for c in (192, 256, 128, 96, 64, 32, 16) if rows % c == 0)
    sets = len(relative)
    return pl.pallas_call(
        functools.partial(proj_kernel, relative, nz, nq, half, chunk),
        out_shape=jax.ShapeDtypeStruct((sets, rows, 2 * rank), dtype),
        in_specs=[HBM, HBM, HBM, HBM, SMEM],
        out_specs=VMEM,
        scratch_shapes=[
            pltpu.VMEM((sets, rows, width), BF),
            pltpu.VMEM((sets, rows, width), BF),
            pltpu.VMEM((width, rank), BF),
            pltpu.VMEM((width, rank), BF),
            pltpu.SemaphoreType.DMA((2, sets, rows // chunk)),
            pltpu.SemaphoreType.DMA((2,)),
        ],
        compiler_params=params(16),
        cost_estimate=pl.CostEstimate(
            flops=4 * sets * rows * width * rank, bytes_accessed=4 * sets * rows * width, transcendentals=0
        ),
        name=f"proj{relative[0]}h{half}",
    )(act, grad, w_in, w_out, lengths)


def kron_kernel(nz, nq, seq, half, lengths, *refs):
    count = len(refs) - nz - 1
    parts, outs, scratch = refs[:count], refs[count : count + nz], refs[-1]
    z = lax.axis_index("feat")
    rank = parts[0].shape[1] // 2
    offset = jnp.int32(0)
    for j in range(nq):
        length = lengths[(half * nz + z) * nq + j]
        rows = pl.ds(pl.multiple_of(offset * TOK, TOK), seq)
        total = parts[0][rows, :].astype(F32)
        for part in parts[1:]:
            total = total + part[rows, :].astype(F32)
        tokens = lax.broadcasted_iota(jnp.int32, total.shape, 0)
        total = jnp.where(tokens < length, total, 0.0)
        high = total.astype(BF)
        low = (total - high.astype(F32)).astype(BF)
        a_hi, a_lo = high[:, :rank], low[:, :rank]
        g_hi, g_lo = high[:, rank:], low[:, rank:]
        left = jnp.concatenate([g_hi, g_hi, g_lo], axis=0)
        right = jnp.concatenate([a_hi, a_lo, a_hi], axis=0)
        outer = lax.dot_general(left, right, (((0,), (0,)), ((), ())), preferred_element_type=F32)
        scratch[:, j, :] = outer * (1.0 / jnp.sqrt(jnp.float32(seq)))
        offset = offset + blocks_of(length)
    share = rank // nz
    for e in range(nz):
        outs[e][...] = scratch[pl.ds((z ^ e) * share, share), :, :].astype(BF)


def kron_of(nz, seq, half, lengths, parts):
    rank = parts[0].shape[1] // 2
    nq = parts[0].shape[0] // seq
    share = rank // nz
    return pl.pallas_call(
        functools.partial(kron_kernel, nz, nq, seq, half),
        out_shape=[jax.ShapeDtypeStruct((share, nq, rank), BF)] * nz,
        in_specs=[SMEM] + [VMEM] * len(parts),
        out_specs=[VMEM] * nz,
        scratch_shapes=[pltpu.VMEM((rank, nq, rank), F32)],
        compiler_params=params(16),
        cost_estimate=pl.CostEstimate(
            flops=6 * nq * seq * rank * rank, bytes_accessed=8 * nq * seq * rank * nz, transcendentals=0
        ),
        name=f"kronh{half}",
    )(lengths, *parts)


def precond_kernel(nz, hess, *refs):
    parts, outs, lhs = refs[:nz], refs[nz : nz + 2], refs[nz + 2]
    z = lax.axis_index("feat")
    blocks, order, _ = hess.shape
    share, nq, rank = parts[0].shape
    per = order // rank
    rows = lhs.shape[0]
    row = lax.broadcasted_iota(jnp.int32, (rows, rows), 0)
    column = lax.broadcasted_iota(jnp.int32, (rows, rows), 1)
    source = lax.div(column, nq) ^ z
    select = (row == source * nq + lax.rem(column, nq)).astype(F32).astype(BF)
    wide = outs[0].shape[1]
    for b in range(blocks):
        for e in range(nz):
            for i in range(per):
                lhs[e * nq : (e + 1) * nq, i * rank : (i + 1) * rank] = parts[e][b * per + i].astype(F32)
        ordered = jnp.dot(select, lhs[...].astype(BF), preferred_element_type=F32).astype(BF)
        result = jnp.dot(ordered, hess[b], preferred_element_type=F32).astype(BF)
        start = b * order
        outs[start // wide][:, start % wide : start % wide + order] = result


def precondition(nz, half, hess, parts):
    blocks, order, _ = hess.shape
    share, nq, rank = parts[0].shape
    queries = nq * nz
    wide = blocks * order // 2
    return pl.pallas_call(
        functools.partial(precond_kernel, nz),
        out_shape=[jax.ShapeDtypeStruct((queries, wide), BF)] * 2,
        in_specs=[VMEM] * (1 + nz),
        out_specs=[VMEM] * 2,
        scratch_shapes=[pltpu.VMEM((queries, order), F32)],
        compiler_params=params(16),
        cost_estimate=pl.CostEstimate(
            flops=2 * queries * blocks * order * order, bytes_accessed=2 * blocks * order * order, transcendentals=0
        ),
        name=f"precondh{half}",
    )(hess, *parts)


def score_kernel(nz, nr, tile, train, *refs):
    pieces, sent, kept, lhs = refs[:4], refs[4], refs[5], refs[6]
    z, r = lax.axis_index("feat"), lax.axis_index("rows")
    block, wide = pieces[0].shape[1:]
    width = (nr // 2).bit_length() - 1
    for e in range(nr // 2):
        mirrored = sum(((e >> b) & 1) << (width - 1 - b) for b in range(width))
        for k, piece in enumerate(pieces):
            rows = pl.ds(pl.multiple_of((r ^ (2 * e + k // 2)) * block, block), block)
            side = k % 2
            lhs[rows, side * wide : (side + 1) * wide] = piece[mirrored if side else e]

    count = lhs.shape[0] // nz

    def step(i, carry):
        cols = pl.ds(pl.multiple_of(i * tile, tile), tile)
        acc = lax.dot_general(lhs[...], train[cols, :], (((1,), (1,)), ((), ())), preferred_element_type=F32)
        for e in range(nz):
            mine = z ^ e
            value = acc[0:count, :]
            for k in range(1, nz):
                value = jnp.where(mine == k, acc[k * count : (k + 1) * count, :], value)
            if e & 1:
                sent[e // 2, :, cols] = value.astype(BF)
            else:
                kept[e // 2, :, cols] = value
        return carry

    lax.fori_loop(0, train.shape[0] // tile, step, 0)


def scores_of(nz, nr, half, train, pieces):
    rows, width = train.shape
    queries = nr * pieces[0].shape[1]
    tile = next(t for t in (512, 256, 128) if rows % t == 0)
    count = queries // nz
    return pl.pallas_call(
        functools.partial(score_kernel, nz, nr, tile),
        out_shape=[
            jax.ShapeDtypeStruct((nz // 2, count, rows), BF),
            jax.ShapeDtypeStruct((nz // 2, count, rows), F32),
        ],
        in_specs=[VMEM] * 5,
        out_specs=[VMEM] * 2,
        scratch_shapes=[pltpu.VMEM((queries, width), BF)],
        compiler_params=params(20),
        cost_estimate=pl.CostEstimate(
            flops=2 * queries * rows * width, bytes_accessed=2 * rows * width, transcendentals=0
        ),
        name=f"scoresh{half}",
    )(train, *pieces)


def on_device(nz, nr, activations, out_grads, proj_in, proj_out, lengths, hess_tiles, train_grads):
    seq = activations.shape[1]
    rank = proj_in.shape[1]
    feat_bits = [1 << b for b in range(nz.bit_length() - 1)]
    row_bits = [1 << b for b in range(1, nr.bit_length() - 1)]

    def across(x, axis, size, e):
        return lax.ppermute(x, axis, [(i, i ^ e) for i in range(size)])

    def over_feat(x, e):
        return across(x, "feat", nz, e)

    def over_rows(x, e):
        return across(x, "rows", nr, e)

    def reduce_scatter(sent, kept):
        got = over_feat(sent, 1)
        for bit in feat_bits[1:]:
            total = [kept[k] + got[k].astype(F32) for k in range(kept.shape[0])]
            got = over_feat(jnp.stack([t.astype(BF) for t in total[1::2]]), bit)
            kept = jnp.stack(total[0::2])
        return kept[0], got[0]

    weights = (activations, out_grads, proj_in, proj_out, lengths)
    odd = [e for e in range(nz) if e & 1]
    even = [e for e in range(nz) if not e & 1]
    columns = []
    sent = [project(odd, nz, h, *weights, BF) for h in range(HALVES)]
    kept = [project(even, nz, h, *weights, F32) for h in range(HALVES)]
    for h in range(HALVES):
        krons = kron_of(nz, seq, h, lengths, list(reduce_scatter(sent[h], kept[h])))
        pieces = [krons[0]] + [over_feat(krons[e], e) for e in range(1, nz)]
        first, second = (x[None] for x in precondition(nz, h, hess_tiles, pieces))
        for bit, other in zip(row_bits, reversed(row_bits), strict=True):
            got_first, got_second = over_rows(first, bit), over_rows(second, other)
            first = jnp.concatenate([first, got_first], axis=0)
            second = jnp.concatenate([second, got_second], axis=0)
        gathered = [first, second, over_rows(first, 1), over_rows(second, 1)]
        own, other = reduce_scatter(*scores_of(nz, nr, h, train_grads, gathered))
        columns.append((own + other.astype(F32)) * (1.0 / rank))
    groups = nr // nz
    columns = [c.reshape(groups, -1, c.shape[1]) for c in columns]
    return jnp.concatenate(columns, axis=1).reshape(-1, columns[0].shape[2])


def solution(mesh):
    nz, nr = mesh.shape["feat"], mesh.shape["rows"]
    return jax.shard_map(
        functools.partial(on_device, nz, nr),
        mesh=mesh,
        in_specs=(
            P("rows", None, "feat"),
            P("rows", None, "feat"),
            P("feat", None),
            P("feat", None),
            P("rows"),
            P("feat", None, None),
            P("rows", "feat"),
        ),
        out_specs=P("feat", "rows"),
        check_vma=False,
    )
```
